32 devices in a mesh: grp: 2 (over y), ccd: 4 (over z), row: 2 (over x), amp: 2 (over core).
Axes of the slice: x: 2, y: 2, z: 4, core: 2. Of those that a mesh axis runs over, the one named last changes fastest.
Arguments:
- science: float32 [8, 512, 1024], P(('grp', 'ccd'), 'row', 'amp'), parts along dimension 0, may hold values from -6 to 6
- template: bfloat16 [8, 2, 2, 8, 32, 512], P(('grp', 'ccd'), 'row', 'amp'), parts along dimension 0, may hold values from -6 to 6
- owners: int32 [8, 2, 2, 8, 1], P(('grp', 'ccd'), 'row', 'amp'), parts along dimension 0, may hold values from 0 to 3; in each aligned block of 8 rows (0 to 7, 8 to 15, ..., all dimensions but the last counted through in order) at most 2 rows name the same one
- patch_strip: int32 [8, 2, 2, 8], P(('grp', 'ccd'), 'row', 'amp'), parts along dimension 0, may hold values from 0 to 7
- shifts: int32 [8, 2, 2, 2, 8], P(('grp', 'ccd'), 'row', 'amp'), parts along dimension 0, may hold values from -3 to 3
- fractions: float32 [8, 2, 2, 2, 8], P(('grp', 'ccd'), 'row', 'amp'), parts along dimension 0, may hold values from 0.05 to 0.95
- coefs: float32 [8, 3, 9], P(('grp', 'ccd')), parts along dimension 0, may hold values from -3 to 3
Outputs:
- difference: float32 [8, 512, 1024], P(('grp', 'ccd'), 'row', 'amp'), parts along dimension 0
- stack: float32 [8, 2, 2, 8, 32, 512], P(('grp', 'ccd'), 'row', 'amp'), parts along dimension 0
The draws below stay inside these ranges and needn't reach their ends.
There are 2 independent parts, one for each index of `grp`. The reference program is written for one: setup_inputs(seed, part) draws one part's arguments, and reference() takes and returns one part's arrays. A program takes and returns all parts, laid end to end along the dimension named above; each array names one. Nothing has to cross between parts.
Inputs may be any that keep to these rules, and one draw needn't show every extreme that they name: Among the 8 strips of one device's block no owner is named more than 2 times, and some block names one owner exactly 2 times in every draw; owners lie in the same row band and column half as the block.
All inputs are finite; a program needn't handle non-finite values.
Results may differ from the reference program's by a relative error of at most 0.0057.
Values may be sent and summed in bfloat16 or wider, within the bound.
A program may use at most 64 MiB of HBM per device.

```python
import math
import jax
import jax.numpy as jnp
import numpy as np
from jax import lax

BAND = 256
HALF = 512
STRIP_ROWS = 32
RADIUS = 9
CCDS = 4
BANDS = 2
HALVES = 2
STRIPS = 8
CAP = 2
IMG_ROWS = 512
IMG_COLS = 1024


def with_ends(array, key, smallest, largest):
    index_at = [jax.random.randint(jax.random.fold_in(key, axis), (), 0, length) for axis, length in enumerate(array.shape)]
    widest = array.shape.index(max(array.shape))
    neighbour = index_at[:widest] + [(index_at[widest] + 1) % array.shape[widest]] + index_at[widest + 1:]
    return array.at[tuple(index_at)].set(smallest).at[tuple(neighbour)].set(largest)


def levels(key, dims, shards, smallest, largest):
    gain = 1.0
    for axis_at, shards_of in shards:
        steps = jax.random.uniform(jax.random.fold_in(jax.random.fold_in(key, 6), axis_at), (shards_of,), jnp.float32, smallest / len(shards), largest / len(shards))
        gain = gain * jnp.repeat(jnp.exp(steps), dims[axis_at] // shards_of).reshape((-1,) + (1,) * (len(dims) - 1 - axis_at))
    return gain


def shared_out(own_key, own, number, rows, number_of, top, limit, lean):
    ranking = jax.random.permutation(own_key, number_of)
    packed, common = portions_of(number_of, rows * top, limit, lean, True), portions_of(number_of, rows * top, limit, lean, False)
    places = jnp.arange(number_of)

    def named(sizes, turn):
        used = int((sizes > 0).sum())
        fixed = max(1, used // 4)
        passed = fixed + (places - fixed + turn * (used - fixed)) % max(1, number_of - fixed)
        return jnp.zeros((number_of,), jnp.int32).at[ranking[jnp.where(places < fixed, places, passed)]].set(jnp.asarray(sizes, jnp.int32))

    sizes = jnp.where(number % 4 == 0, named(packed, number // 4), named(common, number - number // 4 - 1))
    mixed = jax.random.permutation(jax.random.fold_in(own, 3), number_of)
    donor, receiver = mixed[0:number_of // 2 * 2:2], mixed[1:number_of // 2 * 2:2]
    room = jnp.minimum(sizes[donor] - 1, limit - sizes[receiver]) // 2
    room = jnp.where((donor == ranking[0]) | (receiver == ranking[0]) | (sizes[receiver] == 0), 0, jnp.maximum(room, 0))
    passed = jax.random.randint(jax.random.fold_in(own, 4), (number_of // 2,), 0, 1 << 20) % (room + 1)
    sizes = sizes.at[donor].add(-passed).at[receiver].add(passed)
    members = jnp.searchsorted(jnp.cumsum(sizes), jnp.arange(rows * top), side="right").astype(jnp.int32)
    listing = members.reshape(top, rows).T
    listing = listing[jax.random.permutation(jax.random.fold_in(own, 1), rows)]
    turn = jax.random.randint(jax.random.fold_in(own, 2), (rows, 1), 0, top)
    return jnp.take_along_axis(listing, (jnp.arange(top)[None, :] + turn) % top, axis=1)


def portions_of(count, total, reach, skew, full):
    weights = [(1 << 20) // math.isqrt(rank ** skew) + 1 for rank in range(1, count + 1)]
    largest = reach if full else min(reach, max(-(-total // count), total * weights[0] // sum(weights)))
    least = 1 if total - largest >= count - 1 else 0
    given, spare = [largest] + [least] * (count - 1), total - largest - least * (count - 1)
    while spare > 0:
        movable = [i for i in range(1, count) if given[i] < largest] or [i for i in range(1, count) if given[i] < reach]
        pool, left = sum([weights[i] for i in movable]), spare
        for i in movable:
            addition = min(reach - given[i], max(1, left * weights[i] // pool), spare)
            given[i] = given[i] + addition
            spare = spare - addition
    return np.array(given)


def centred(own_key, extent, scale, bound, split=(), held_as=jnp.bfloat16):
    entries = scale * jax.random.normal(own_key, extent, jnp.float32)
    if split:
        entries = entries * levels(own_key, extent, split, -0.22, 0.18)
    return jnp.clip(entries, -bound, bound).astype(held_as)


def setup_inputs(seed: int = 0, part: int = 0) -> dict:
    keys = jax.random.split(jax.random.key(seed), 8)
    own_keys = jax.random.split(jax.random.fold_in(keys[7], part), 8)
    science = centred(own_keys[0], (CCDS, IMG_ROWS, IMG_COLS), 1.0, 6.0, ((0, 4), (1, 2), (2, 2)), jnp.float32)
    template = centred(own_keys[1], (CCDS, BANDS, HALVES, STRIPS, STRIP_ROWS, HALF), 1.0, 6.0, ((0, 4), (1, 2), (2, 2)))
    owners_keys = jax.random.split(jax.random.fold_in(own_keys[2], 1), CCDS * BANDS * HALVES * STRIPS // STRIPS)
    owners_turns = jax.random.permutation(jax.random.fold_in(own_keys[2], 3), CCDS * BANDS * HALVES * STRIPS // STRIPS)
    owners = jax.vmap(lambda own, number: shared_out(jax.random.fold_in(own_keys[2], 2), own, number, STRIPS, CCDS, 1, CAP, 2))(owners_keys, owners_turns).reshape((CCDS, BANDS, HALVES, STRIPS, 1))
    patch_strip = with_ends(jax.random.randint(own_keys[3], (CCDS, BANDS, HALVES, STRIPS), 0, STRIPS), jax.random.fold_in(own_keys[3], 1), 0, STRIPS - 1).astype(jnp.int32)
    shifts = with_ends(jax.random.randint(own_keys[4], (CCDS, BANDS, HALVES, 2, STRIPS), -3, 4), jax.random.fold_in(own_keys[4], 1), -3, 3).astype(jnp.int32)
    fractions = jnp.clip(0.05 + 0.9 * jax.random.uniform(own_keys[5], (CCDS, BANDS, HALVES, 2, STRIPS), jnp.float32) ** levels(own_keys[5], (CCDS, BANDS, HALVES, 2, STRIPS), ((0, 4), (1, 2), (2, 2)), -0.2, 0.2), 0.05, 0.95)
    coefs = centred(own_keys[6], (CCDS, 3, 9), 0.5, 3.0, ((0, 4),), jnp.float32)
    return {"science": science, "template": template, "owners": owners, "patch_strip": patch_strip, "shifts": shifts, "fractions": fractions, "coefs": coefs}


tap_margin = 6


def lanczos_taps(fraction):
    offsets = jnp.arange(-2, 4).astype(jnp.float32)
    spread = offsets[None, :] - fraction[:, None]
    return (jnp.sinc(spread) * jnp.sinc(spread / 3.0)).astype(jnp.bfloat16)


def kernel_table():
    support = jnp.arange(-RADIUS, RADIUS + 1).astype(jnp.float32)
    narrow = jnp.exp(-support * support / 4.5)
    slope = support * jnp.exp(-support * support / 12.5)
    broad = jnp.exp(-support * support / 40.5)
    return jnp.stack([narrow / jnp.sum(narrow), slope / jnp.sum(jnp.abs(slope)), broad / jnp.sum(broad)]).astype(jnp.bfloat16)


def strip_operator(taps, shift, strip_rows):
    out_rows = jnp.arange(strip_rows).astype(jnp.int32)[None, :, None]
    src_rows = jnp.arange(strip_rows).astype(jnp.int32)[None, None, :]
    offset = src_rows - out_rows - shift.astype(jnp.int32)[:, None, None]
    table = jnp.zeros(offset.shape, jnp.bfloat16)
    for which in range(6):
        table = jnp.where(offset == which - 2, taps[:, which][:, None, None], table)
    return table


def shift_columns(values, taps, starts, width):
    def one_strip(block, tap_row, start_row):
        total = jnp.zeros((block.shape[0], width), jnp.float32)
        for which in range(6):
            moved = lax.dynamic_slice_in_dim(block, start_row[which], width, 1)
            total = total + tap_row[which].astype(jnp.float32) * moved.astype(jnp.float32)
        return total
    return jax.vmap(one_strip)(values, taps, starts)


def tap_steps():
    return (jnp.arange(6) - 2).astype(jnp.int32)


def forward_warp(block, shift_pair, fraction_pair):
    strip_rows = block.shape[1]
    width = block.shape[2]
    row_taps = lanczos_taps(fraction_pair[0])
    col_taps = lanczos_taps(fraction_pair[1])
    operator = strip_operator(row_taps, shift_pair[0], strip_rows)
    rows_done = jnp.einsum("qik,qkz->qiz", operator.astype(jnp.float32), block.astype(jnp.float32)).astype(jnp.bfloat16)
    starts = (tap_margin + shift_pair[1].astype(jnp.int32)[:, None] + tap_steps()[None, :]).astype(jnp.int32)
    padded = jnp.pad(rows_done, ((0, 0), (0, 0), (tap_margin, tap_margin)))
    return shift_columns(padded, col_taps, starts, width).astype(jnp.bfloat16)


def backward_warp(block, shift_pair, fraction_pair):
    strip_rows = block.shape[1]
    width = block.shape[2]
    row_taps = lanczos_taps(fraction_pair[0])
    col_taps = lanczos_taps(fraction_pair[1])
    operator = strip_operator(row_taps, shift_pair[0], strip_rows)
    starts = (tap_margin - shift_pair[1].astype(jnp.int32)[:, None] - tap_steps()[None, :]).astype(jnp.int32)
    padded = jnp.pad(block, ((0, 0), (0, 0), (tap_margin, tap_margin)))
    columns_back = shift_columns(padded, col_taps, starts, width).astype(jnp.bfloat16)
    return jnp.einsum("qik,qiz->qkz", operator.astype(jnp.float32), columns_back.astype(jnp.float32))


def reference(science, template, owners, patch_strip, shifts, fractions, coefs):
    kernels = kernel_table()
    owner_all = owners[..., 0]
    band_index = jnp.arange(BANDS).astype(jnp.int32)[None, :, None, None]
    half_index = jnp.arange(HALVES).astype(jnp.int32)[None, None, :, None]
    chosen_all = template[owner_all, band_index, half_index, patch_strip]
    row_place = (jnp.arange(IMG_ROWS) + 0.5) / IMG_ROWS * 2.0 - 1.0
    col_place = (jnp.arange(IMG_COLS) + 0.5) / IMG_COLS * 2.0 - 1.0
    blocks = BANDS * HALVES
    width = 2 * RADIUS + 1

    def one_ccd(inputs):
        chosen, image_science, shift_ccd, fraction_ccd, coef_ccd = inputs
        chosen_flat = chosen.reshape(blocks, STRIPS, STRIP_ROWS, HALF)
        shift_flat = shift_ccd.reshape(blocks, 2, STRIPS)
        fraction_flat = fraction_ccd.reshape(blocks, 2, STRIPS)
        warped = jax.vmap(forward_warp)(chosen_flat, shift_flat, fraction_flat)
        image = warped.reshape(BANDS, HALVES, BAND, HALF).transpose(0, 2, 1, 3).reshape(IMG_ROWS, IMG_COLS)
        padded = jnp.pad(image, RADIUS)
        model = jnp.zeros((IMG_ROWS, IMG_COLS), jnp.float32)
        for first in range(3):
            across = jnp.zeros((IMG_ROWS, IMG_COLS + 2 * RADIUS), jnp.float32)
            for offset in range(width):
                across = across + kernels[first, offset].astype(jnp.float32) * padded[offset:offset + IMG_ROWS, :].astype(jnp.float32)
            across = across.astype(jnp.bfloat16)
            for second in range(3):
                term = jnp.zeros((IMG_ROWS, IMG_COLS), jnp.float32)
                for offset in range(width):
                    term = term + kernels[second, offset].astype(jnp.float32) * across[:, offset:offset + IMG_COLS].astype(jnp.float32)
                basis = first * 3 + second
                weight = coef_ccd[0, basis] + coef_ccd[1, basis] * col_place[None, :] + coef_ccd[2, basis] * row_place[:, None]
                model = model + weight * term
        difference = image_science - model
        lowered = difference.astype(jnp.bfloat16).reshape(BANDS, BAND, HALVES, HALF).transpose(0, 2, 1, 3)
        lowered = lowered.reshape(blocks, STRIPS, STRIP_ROWS, HALF)
        contribution = jax.vmap(backward_warp)(lowered, shift_flat, fraction_flat)
        return difference, contribution.reshape(BANDS, HALVES, STRIPS, STRIP_ROWS, HALF)

    differences, contributions = lax.map(one_ccd, (chosen_all, science, shifts, fractions, coefs))
    stack = jnp.zeros(template.shape, jnp.float32).at[owner_all, band_index, half_index, patch_strip].add(contributions)
    return differences, stack
```

```python
import jax
import jax.numpy as jnp
from jax import lax
from jax.sharding import PartitionSpec as P

RADIUS = 9


tap_margin = 6


def padded_2(value, sides, width):
    for axis, dim in sides:
        devices, length = (lax.axis_size(axis), value.shape[dim])
        up = [(i, (i + 1) % devices) for i in range(devices - 1)]
        down = [(j, i) for i, j in up]
        last = lax.slice_in_dim(value, length - width, length, axis=dim)
        first = lax.slice_in_dim(value, 0, width, axis=dim)
        before = lax.ppermute(last, axis, up)
        after = lax.ppermute(first, axis, down)
        value = jnp.concatenate([before, value, after], axis=dim)
    return value


def lanczos_taps(fraction):
    offsets = jnp.arange(-2, 4).astype(jnp.float32)
    spread = offsets[None, :] - fraction[:, None]
    return (jnp.sinc(spread) * jnp.sinc(spread / 3.0)).astype(jnp.bfloat16)


def kernel_table():
    support = jnp.arange(-RADIUS, RADIUS + 1).astype(jnp.float32)
    narrow = jnp.exp(-support * support / 4.5)
    slope = support * jnp.exp(-support * support / 12.5)
    broad = jnp.exp(-support * support / 40.5)
    return jnp.stack(
        [narrow / jnp.sum(narrow), slope / jnp.sum(jnp.abs(slope)), broad / jnp.sum(broad)]
    ).astype(jnp.bfloat16)


def strip_operator(taps, shift, strip_rows):
    out_rows = jnp.arange(strip_rows)[None, :, None]
    src_rows = jnp.arange(strip_rows)[None, None, :]
    offset = src_rows - out_rows - shift[:, None, None]
    table = jnp.zeros(offset.shape, jnp.bfloat16)
    for which in range(6):
        table = jnp.where(offset == which - 2, taps[:, which][:, None, None], table)
    return table


def shift_columns(values, taps, starts, width):

    def one_strip(block, tap_row, start_row):
        total = jnp.zeros((block.shape[0], width), jnp.float32)
        for which in range(6):
            moved = lax.dynamic_slice_in_dim(block, start_row[which], width, 1)
            total = total + tap_row[which].astype(jnp.float32) * moved.astype(jnp.float32)
        return total

    return jax.vmap(one_strip)(values, taps, starts)


def shift_weights(taps, shift):
    offsets = jnp.arange(-5, 7)[None, :, None]
    steps = (jnp.arange(6) - 2)[None, None, :]
    hit = offsets == shift[:, None, None] + steps
    return jnp.sum(jnp.where(hit, taps.astype(jnp.float32)[:, None, :], 0.0), axis=2)


def static_shift(values, weights, sign, width):
    wide = jnp.pad(values, ((0, 0), (0, 0), (tap_margin, tap_margin)))
    total = jnp.zeros((values.shape[0], values.shape[1], width), jnp.float32)
    for which in range(12):
        start = tap_margin + sign * (which - 5)
        moved = lax.slice_in_dim(wide, start, start + width, axis=2).astype(jnp.float32)
        total = total + weights[:, which][:, None, None] * moved
    return total


def band_operator(kernel, count):
    out_place = jnp.arange(count)[:, None]
    src_place = jnp.arange(count + 2 * RADIUS)[None, :]
    spacing = src_place - out_place
    table = jnp.zeros(spacing.shape, jnp.bfloat16)
    for offset in range(2 * RADIUS + 1):
        table = jnp.where(spacing == offset, kernel[offset], table)
    return table


def body(science, template, owners, patch_strip, shifts, fractions, coefs):
    ccd_count = lax.axis_size("ccd")
    row_count = lax.axis_size("row")
    amp_count = lax.axis_size("amp")
    band_rows = science.shape[1]
    half_cols = science.shape[2]
    strips = template.shape[3]
    strip_rows = template.shape[4]
    strip_size = strip_rows * half_cols
    capacity = max(2, strips // ccd_count)
    owner_list = owners.reshape(strips)
    strip_list = patch_strip.reshape(strips)
    earlier = jnp.arange(strips)[None, :] < jnp.arange(strips)[:, None]
    same_owner = owner_list[None, :] == owner_list[:, None]
    place_rank = jnp.sum(jnp.where(earlier & same_owner, 1, 0), axis=1).astype(jnp.int32)
    slot_index = owner_list * capacity + place_rank
    slot_match = jnp.arange(ccd_count * capacity)[:, None] == slot_index[None, :]
    wanted = jnp.sum(jnp.where(slot_match, strip_list[None, :] + 1, 0), axis=1) - 1
    asked = lax.all_to_all(
        wanted.reshape(ccd_count, capacity), "ccd", split_axis=0, concat_axis=0, tiled=True
    )
    asked_flat = asked.reshape(ccd_count * capacity)
    global_index = owner_list * strips + strip_list
    rows_here = lax.all_gather(template, "ccd", axis=0, tiled=True).reshape(-1, strip_size)
    labels = jnp.arange(rows_here.shape[0])
    select = (global_index[:, None] == labels[None, :]).astype(jnp.bfloat16)
    chosen = jnp.dot(select, rows_here, preferred_element_type=jnp.float32)
    chosen = chosen.astype(jnp.bfloat16)
    chosen = chosen.reshape(strips, strip_rows, half_cols)
    row_taps = lanczos_taps(fractions[0, 0, 0, 0])
    col_taps = lanczos_taps(fractions[0, 0, 0, 1])
    row_shift = shifts[0, 0, 0, 0]
    col_shift = shifts[0, 0, 0, 1]
    tap_steps = jnp.arange(6) - 2
    row_warp = strip_operator(row_taps, row_shift, strip_rows)
    rows_done = jnp.einsum(
        "qik,qkz->qiz", row_warp, chosen, preferred_element_type=jnp.float32
    ).astype(jnp.bfloat16)
    col_weights = shift_weights(col_taps, col_shift)
    warped = static_shift(rows_done, col_weights, 1, half_cols).astype(jnp.bfloat16)
    image = warped.reshape(band_rows, half_cols)
    padded = padded_2(image, (("row", 0), ("amp", 1)), RADIUS)
    kernels = kernel_table()
    row_place = (
        (lax.axis_index("row") * band_rows + jnp.arange(band_rows) + 0.5)
        / (band_rows * row_count)
        * 2.0
        - 1.0
    )[:, None]
    col_place = (
        (lax.axis_index("amp") * half_cols + jnp.arange(half_cols) + 0.5)
        / (half_cols * amp_count)
        * 2.0
        - 1.0
    )[None, :]
    coef_block = coefs[0]
    row_mats = jnp.concatenate([band_operator(kernels[kind], band_rows) for kind in range(3)], axis=0)
    column_mats = jnp.concatenate(
        [band_operator(kernels[kind], half_cols).T for kind in range(3)], axis=1
    )
    row_mats, column_mats = lax.optimization_barrier((row_mats, column_mats))
    across_all = jnp.dot(row_mats, padded, preferred_element_type=jnp.float32).astype(jnp.bfloat16)
    terms = jnp.dot(across_all, column_mats, preferred_element_type=jnp.float32)
    model = jnp.zeros((band_rows, half_cols), jnp.float32)
    for first in range(3):
        for second in range(3):
            basis = first * 3 + second
            term = terms[first * band_rows:(first + 1) * band_rows, second * half_cols:(second + 1) * half_cols]
            weight = (
                coef_block[0, basis]
                + coef_block[1, basis] * col_place
                + coef_block[2, basis] * row_place
            )
            model = model + weight * term
    difference = science[0] - model
    lowered = difference.astype(jnp.bfloat16).reshape(strips, strip_rows, half_cols)
    columns_back = static_shift(lowered, col_weights, -1, half_cols).astype(jnp.bfloat16)
    contribution = jnp.einsum(
        "qik,qiz->qkz", row_warp, columns_back, preferred_element_type=jnp.float32
    )
    outgoing_back = (
        jnp.zeros((ccd_count * capacity, strip_size), jnp.float32)
        .at[slot_index]
        .set(contribution.reshape(strips, strip_size))
    )
    returned = lax.all_to_all(
        outgoing_back.reshape(ccd_count, capacity, strip_size),
        "ccd",
        split_axis=0,
        concat_axis=0,
        tiled=True,
    )
    owner_select = (asked_flat[:, None] == jnp.arange(strips)[None, :]).astype(jnp.float32)
    stack = jnp.einsum(
        "sp,sz->pz",
        owner_select,
        returned.reshape(ccd_count * capacity, strip_size),
        precision=lax.Precision.HIGHEST,
    )
    return (difference[None], stack.reshape(template.shape))


def solution(mesh):
    return jax.shard_map(
        body,
        mesh=mesh,
        in_specs=(
            P(("grp", "ccd"), "row", "amp"),
            P(("grp", "ccd"), "row", "amp", None, None, None),
            P(("grp", "ccd"), "row", "amp", None, None),
            P(("grp", "ccd"), "row", "amp", None),
            P(("grp", "ccd"), "row", "amp", None, None),
            P(("grp", "ccd"), "row", "amp", None, None),
            P(("grp", "ccd"), None, None),
        ),
        out_specs=(
            P(("grp", "ccd"), "row", "amp"),
            P(("grp", "ccd"), "row", "amp", None, None, None),
        ),
        check_vma=False,
    )
```

```python
import jax
import jax.numpy as jnp
from jax import lax
from jax.sharding import PartitionSpec as P

RADIUS = 9


tap_margin = 6


def padded_2(value, sides, width):
    for axis, dim in sides:
        devices, length = (lax.axis_size(axis), value.shape[dim])
        up = [(i, (i + 1) % devices) for i in range(devices - 1)]
        down = [(j, i) for i, j in up]
        last = lax.slice_in_dim(value, length - width, length, axis=dim)
        first = lax.slice_in_dim(value, 0, width, axis=dim)
        before = lax.ppermute(last, axis, up)
        after = lax.ppermute(first, axis, down)
        value = jnp.concatenate([before, value, after], axis=dim)
    return value


def lanczos_taps(fraction):
    offsets = jnp.arange(-2, 4).astype(jnp.float32)
    spread = offsets[None, :] - fraction[:, None]
    return (jnp.sinc(spread) * jnp.sinc(spread / 3.0)).astype(jnp.bfloat16)


def kernel_table():
    support = jnp.arange(-RADIUS, RADIUS + 1).astype(jnp.float32)
    narrow = jnp.exp(-support * support / 4.5)
    slope = support * jnp.exp(-support * support / 12.5)
    broad = jnp.exp(-support * support / 40.5)
    return jnp.stack(
        [narrow / jnp.sum(narrow), slope / jnp.sum(jnp.abs(slope)), broad / jnp.sum(broad)]
    ).astype(jnp.bfloat16)


def strip_operator(taps, shift, strip_rows):
    out_rows = jnp.arange(strip_rows)[None, :, None]
    src_rows = jnp.arange(strip_rows)[None, None, :]
    offset = src_rows - out_rows - shift[:, None, None]
    table = jnp.zeros(offset.shape, jnp.bfloat16)
    for which in range(6):
        table = jnp.where(offset == which - 2, taps[:, which][:, None, None], table)
    return table


def shift_columns(values, taps, starts, width):

    def one_strip(block, tap_row, start_row):
        total = jnp.zeros((block.shape[0], width), jnp.float32)
        for which in range(6):
            moved = lax.dynamic_slice_in_dim(block, start_row[which], width, 1)
            total = total + tap_row[which].astype(jnp.float32) * moved.astype(jnp.float32)
        return total

    return jax.vmap(one_strip)(values, taps, starts)


def shift_weights(taps, shift):
    offsets = jnp.arange(-5, 7)[None, :, None]
    steps = (jnp.arange(6) - 2)[None, None, :]
    hit = offsets == shift[:, None, None] + steps
    return jnp.sum(jnp.where(hit, taps.astype(jnp.float32)[:, None, :], 0.0), axis=2)


def static_shift(values, weights, sign, width):
    wide = jnp.pad(values, ((0, 0), (0, 0), (tap_margin, tap_margin)))
    total = jnp.zeros((values.shape[0], values.shape[1], width), jnp.float32)
    for which in range(12):
        start = tap_margin + sign * (which - 5)
        moved = lax.slice_in_dim(wide, start, start + width, axis=2).astype(jnp.float32)
        total = total + weights[:, which][:, None, None] * moved
    return total


def band_operator(kernel, count):
    line = jnp.concatenate([kernel, jnp.zeros((count,), kernel.dtype)])
    width = count + 2 * RADIUS
    flat = jnp.tile(line, count)[: count * width]
    return flat.reshape(count, width)


def body(science, template, owners, patch_strip, shifts, fractions, coefs):
    ccd_count = lax.axis_size("ccd")
    row_count = lax.axis_size("row")
    amp_count = lax.axis_size("amp")
    band_rows = science.shape[1]
    half_cols = science.shape[2]
    strips = template.shape[3]
    strip_rows = template.shape[4]
    strip_size = strip_rows * half_cols
    capacity = max(2, strips // ccd_count)
    owner_list = owners.reshape(strips)
    strip_list = patch_strip.reshape(strips)
    earlier = jnp.arange(strips)[None, :] < jnp.arange(strips)[:, None]
    same_owner = owner_list[None, :] == owner_list[:, None]
    place_rank = jnp.sum(jnp.where(earlier & same_owner, 1, 0), axis=1).astype(jnp.int32)
    slot_index = owner_list * capacity + place_rank
    slot_match = jnp.arange(ccd_count * capacity)[:, None] == slot_index[None, :]
    wanted = jnp.sum(jnp.where(slot_match, strip_list[None, :] + 1, 0), axis=1) - 1
    asked = lax.all_to_all(
        wanted.reshape(ccd_count, capacity), "ccd", split_axis=0, concat_axis=0, tiled=True
    )
    asked_flat = asked.reshape(ccd_count * capacity)
    global_index = owner_list * strips + strip_list
    rows_here = lax.all_gather(template, "ccd", axis=0, tiled=True).reshape(-1, strip_size)
    labels = jnp.arange(rows_here.shape[0])
    select = (global_index[:, None] == labels[None, :]).astype(jnp.bfloat16)
    chosen = jnp.dot(select, rows_here, preferred_element_type=jnp.float32)
    chosen = chosen.astype(jnp.bfloat16)
    chosen = chosen.reshape(strips, strip_rows, half_cols)
    row_taps = lanczos_taps(fractions[0, 0, 0, 0])
    col_taps = lanczos_taps(fractions[0, 0, 0, 1])
    row_shift = shifts[0, 0, 0, 0]
    col_shift = shifts[0, 0, 0, 1]
    tap_steps = jnp.arange(6) - 2
    row_warp = strip_operator(row_taps, row_shift, strip_rows)
    rows_done = jnp.einsum(
        "qik,qkz->qiz", row_warp, chosen, preferred_element_type=jnp.float32
    ).astype(jnp.bfloat16)
    rows_done = lax.optimization_barrier(rows_done)
    col_weights = shift_weights(col_taps, col_shift)
    warped = static_shift(rows_done, col_weights, 1, half_cols).astype(jnp.bfloat16)
    image = warped.reshape(band_rows, half_cols)
    padded = padded_2(image, (("row", 0), ("amp", 1)), RADIUS)
    kernels = kernel_table()
    row_place = (
        (lax.axis_index("row") * band_rows + jnp.arange(band_rows) + 0.5)
        / (band_rows * row_count)
        * 2.0
        - 1.0
    )[:, None]
    col_place = (
        (lax.axis_index("amp") * half_cols + jnp.arange(half_cols) + 0.5)
        / (half_cols * amp_count)
        * 2.0
        - 1.0
    )[None, :]
    coef_block = coefs[0]
    row_mats = jnp.concatenate([band_operator(kernels[kind], band_rows) for kind in range(3)], axis=0)
    column_mats = jnp.concatenate(
        [band_operator(kernels[kind], half_cols).T for kind in range(3)], axis=1
    )
    row_mats, column_mats = lax.optimization_barrier((row_mats, column_mats))
    across_all = jnp.dot(row_mats, padded, preferred_element_type=jnp.float32).astype(jnp.bfloat16)
    terms = jnp.dot(across_all, column_mats, preferred_element_type=jnp.float32)
    model = jnp.zeros((band_rows, half_cols), jnp.float32)
    for first in range(3):
        for second in range(3):
            basis = first * 3 + second
            term = terms[first * band_rows:(first + 1) * band_rows, second * half_cols:(second + 1) * half_cols]
            weight = (
                coef_block[0, basis]
                + coef_block[1, basis] * col_place
                + coef_block[2, basis] * row_place
            )
            model = model + weight * term
    difference = science[0] - model
    lowered = difference.astype(jnp.bfloat16).reshape(strips, strip_rows, half_cols)
    lowered = lax.optimization_barrier(lowered)
    columns_back = static_shift(lowered, col_weights, -1, half_cols).astype(jnp.bfloat16)
    contribution = jnp.einsum(
        "qik,qiz->qkz", row_warp, columns_back, preferred_element_type=jnp.float32
    )
    outgoing_back = (
        jnp.zeros((ccd_count * capacity, strip_size), jnp.float32)
        .at[slot_index]
        .set(contribution.reshape(strips, strip_size))
    )
    returned = lax.all_to_all(
        outgoing_back.reshape(ccd_count, capacity, strip_size),
        "ccd",
        split_axis=0,
        concat_axis=0,
        tiled=True,
    )
    owner_select = (asked_flat[:, None] == jnp.arange(strips)[None, :]).astype(jnp.float32)
    stack = jnp.einsum(
        "sp,sz->pz",
        owner_select,
        returned.reshape(ccd_count * capacity, strip_size),
        precision=lax.Precision.HIGHEST,
    )
    return (difference[None], stack.reshape(template.shape))


def solution(mesh):
    return jax.shard_map(
        body,
        mesh=mesh,
        in_specs=(
            P(("grp", "ccd"), "row", "amp"),
            P(("grp", "ccd"), "row", "amp", None, None, None),
            P(("grp", "ccd"), "row", "amp", None, None),
            P(("grp", "ccd"), "row", "amp", None),
            P(("grp", "ccd"), "row", "amp", None, None),
            P(("grp", "ccd"), "row", "amp", None, None),
            P(("grp", "ccd"), None, None),
        ),
        out_specs=(
            P(("grp", "ccd"), "row", "amp"),
            P(("grp", "ccd"), "row", "amp", None, None, None),
        ),
        check_vma=False,
    )
```

```python
import jax
import jax.numpy as jnp
from jax import lax
from jax.sharding import PartitionSpec as P

RADIUS = 9


tap_margin = 6


def padded_2(value, sides, width):
    for axis, dim in sides:
        devices, length = (lax.axis_size(axis), value.shape[dim])
        up = [(i, (i + 1) % devices) for i in range(devices - 1)]
        down = [(j, i) for i, j in up]
        last = lax.slice_in_dim(value, length - width, length, axis=dim)
        first = lax.slice_in_dim(value, 0, width, axis=dim)
        before = lax.ppermute(last, axis, up)
        after = lax.ppermute(first, axis, down)
        value = jnp.concatenate([before, value, after], axis=dim)
    return value


def lanczos_taps(fraction):
    offsets = jnp.arange(-2, 4).astype(jnp.float32)
    spread = offsets[None, :] - fraction[:, None]
    return (jnp.sinc(spread) * jnp.sinc(spread / 3.0)).astype(jnp.bfloat16)


def kernel_table():
    support = jnp.arange(-RADIUS, RADIUS + 1).astype(jnp.float32)
    narrow = jnp.exp(-support * support / 4.5)
    slope = support * jnp.exp(-support * support / 12.5)
    broad = jnp.exp(-support * support / 40.5)
    return jnp.stack(
        [narrow / jnp.sum(narrow), slope / jnp.sum(jnp.abs(slope)), broad / jnp.sum(broad)]
    ).astype(jnp.bfloat16)


def strip_operator(taps, shift, strip_rows):
    out_rows = jnp.arange(strip_rows)[None, :, None]
    src_rows = jnp.arange(strip_rows)[None, None, :]
    offset = src_rows - out_rows - shift[:, None, None]
    table = jnp.zeros(offset.shape, jnp.bfloat16)
    for which in range(6):
        table = jnp.where(offset == which - 2, taps[:, which][:, None, None], table)
    return table


def shift_columns(values, taps, starts, width):

    def one_strip(block, tap_row, start_row):
        total = jnp.zeros((block.shape[0], width), jnp.float32)
        for which in range(6):
            moved = lax.dynamic_slice_in_dim(block, start_row[which], width, 1)
            total = total + tap_row[which].astype(jnp.float32) * moved.astype(jnp.float32)
        return total

    return jax.vmap(one_strip)(values, taps, starts)


def shift_weights(taps, shift):
    offsets = jnp.arange(-5, 7)[None, :, None]
    steps = (jnp.arange(6) - 2)[None, None, :]
    hit = offsets == shift[:, None, None] + steps
    return jnp.sum(jnp.where(hit, taps.astype(jnp.float32)[:, None, :], 0.0), axis=2)


def static_shift(values, weights, sign, width):
    wide = jnp.pad(values, ((0, 0), (0, 0), (tap_margin, tap_margin)))
    total = jnp.zeros((values.shape[0], values.shape[1], width), jnp.float32)
    for which in range(12):
        start = tap_margin + sign * (which - 5)
        moved = lax.slice_in_dim(wide, start, start + width, axis=2).astype(jnp.float32)
        total = total + weights[:, which][:, None, None] * moved
    return total


def band_operator(kernel, count):
    line = jnp.concatenate([kernel, jnp.zeros((count,), kernel.dtype)])
    width = count + 2 * RADIUS
    flat = jnp.tile(line, count)[: count * width]
    return flat.reshape(count, width)


def body(science, template, owners, patch_strip, shifts, fractions, coefs):
    ccd_count = lax.axis_size("ccd")
    row_count = lax.axis_size("row")
    amp_count = lax.axis_size("amp")
    band_rows = science.shape[1]
    half_cols = science.shape[2]
    strips = template.shape[3]
    strip_rows = template.shape[4]
    strip_size = strip_rows * half_cols
    capacity = max(2, strips // ccd_count)
    owner_list = owners.reshape(strips)
    strip_list = patch_strip.reshape(strips)
    earlier = jnp.arange(strips)[None, :] < jnp.arange(strips)[:, None]
    same_owner = owner_list[None, :] == owner_list[:, None]
    place_rank = jnp.sum(jnp.where(earlier & same_owner, 1, 0), axis=1).astype(jnp.int32)
    slot_index = owner_list * capacity + place_rank
    global_index = owner_list * strips + strip_list
    rows_here = lax.all_gather(template, "ccd", axis=0, tiled=True).reshape(-1, strip_size)
    labels = jnp.arange(rows_here.shape[0])
    select = (global_index[:, None] == labels[None, :]).astype(jnp.bfloat16)
    chosen = jnp.dot(select, rows_here, preferred_element_type=jnp.float32)
    chosen = chosen.astype(jnp.bfloat16)
    chosen = chosen.reshape(strips, strip_rows, half_cols)
    row_taps = lanczos_taps(fractions[0, 0, 0, 0])
    col_taps = lanczos_taps(fractions[0, 0, 0, 1])
    row_shift = shifts[0, 0, 0, 0]
    col_shift = shifts[0, 0, 0, 1]
    tap_steps = jnp.arange(6) - 2
    row_warp = strip_operator(row_taps, row_shift, strip_rows)
    rows_done = jnp.einsum(
        "qik,qkz->qiz", row_warp, chosen, preferred_element_type=jnp.float32
    ).astype(jnp.bfloat16)
    rows_done = lax.optimization_barrier(rows_done)
    col_weights = shift_weights(col_taps, col_shift)
    warped = static_shift(rows_done, col_weights, 1, half_cols).astype(jnp.bfloat16)
    image = warped.reshape(band_rows, half_cols)
    padded = padded_2(image, (("row", 0), ("amp", 1)), RADIUS)
    row_place = (
        (lax.axis_index("row") * band_rows + jnp.arange(band_rows) + 0.5)
        / (band_rows * row_count)
        * 2.0
        - 1.0
    )[:, None]
    col_place = (
        (lax.axis_index("amp") * half_cols + jnp.arange(half_cols) + 0.5)
        / (half_cols * amp_count)
        * 2.0
        - 1.0
    )[None, :]
    coef_block = coefs[0]
    kernels = kernel_table()
    row_mats = jnp.concatenate([band_operator(kernels[kind], band_rows) for kind in range(3)], axis=0)
    column_mats = jnp.concatenate(
        [band_operator(kernels[kind], half_cols).T for kind in range(3)], axis=1
    )
    across_all = jnp.dot(row_mats, padded, preferred_element_type=jnp.float32).astype(jnp.bfloat16)
    terms = jnp.dot(across_all, column_mats, preferred_element_type=jnp.float32)
    model = jnp.zeros((band_rows, half_cols), jnp.float32)
    for first in range(3):
        for second in range(3):
            basis = first * 3 + second
            term = terms[first * band_rows:(first + 1) * band_rows, second * half_cols:(second + 1) * half_cols]
            weight = (
                coef_block[0, basis]
                + coef_block[1, basis] * col_place
                + coef_block[2, basis] * row_place
            )
            model = model + weight * term
    difference = science[0] - model
    lowered = difference.astype(jnp.bfloat16).reshape(strips, strip_rows, half_cols)
    lowered = lax.optimization_barrier(lowered)
    columns_back = static_shift(lowered, col_weights, -1, half_cols).astype(jnp.bfloat16)
    contribution = jnp.einsum(
        "qik,qiz->qkz", row_warp, columns_back, preferred_element_type=jnp.float32
    )
    tagged = jnp.concatenate(
        [
            contribution.reshape(strips, strip_size),
            jnp.broadcast_to(strip_list.astype(jnp.float32)[:, None] + 1.0, (strips, 128)),
        ],
        axis=1,
    )
    outgoing_back = (
        jnp.zeros((ccd_count * capacity, strip_size + 128), jnp.float32).at[slot_index].set(tagged)
    )
    returned = lax.all_to_all(
        outgoing_back.reshape(ccd_count, capacity, strip_size + 128),
        "ccd",
        split_axis=0,
        concat_axis=0,
        tiled=True,
    )
    returned = returned.reshape(ccd_count * capacity, strip_size + 128)
    asked_flat = returned[:, strip_size].astype(jnp.int32) - 1
    owner_select = (asked_flat[:, None] == jnp.arange(strips)[None, :]).astype(jnp.float32)
    stack = jnp.einsum(
        "sp,sz->pz",
        owner_select,
        returned[:, :strip_size],
        precision=lax.Precision.HIGHEST,
    )
    return (difference[None], stack.reshape(template.shape))


def solution(mesh):
    return jax.shard_map(
        body,
        mesh=mesh,
        in_specs=(
            P(("grp", "ccd"), "row", "amp"),
            P(("grp", "ccd"), "row", "amp", None, None, None),
            P(("grp", "ccd"), "row", "amp", None, None),
            P(("grp", "ccd"), "row", "amp", None),
            P(("grp", "ccd"), "row", "amp", None, None),
            P(("grp", "ccd"), "row", "amp", None, None),
            P(("grp", "ccd"), None, None),
        ),
        out_specs=(
            P(("grp", "ccd"), "row", "amp"),
            P(("grp", "ccd"), "row", "amp", None, None, None),
        ),
        check_vma=False,
    )
```

```python
import jax
import jax.numpy as jnp
from jax import lax
from jax.sharding import PartitionSpec as P

RADIUS = 9


tap_margin = 6


def padded_2(value, sides, width):
    for axis, dim in sides:
        devices, length = (lax.axis_size(axis), value.shape[dim])
        up = [(i, (i + 1) % devices) for i in range(devices - 1)]
        down = [(j, i) for i, j in up]
        last = lax.slice_in_dim(value, length - width, length, axis=dim)
        first = lax.slice_in_dim(value, 0, width, axis=dim)
        before = lax.ppermute(last, axis, up)
        after = lax.ppermute(first, axis, down)
        value = jnp.concatenate([before, value, after], axis=dim)
    return value


def lanczos_taps(fraction):
    offsets = jnp.arange(-2, 4).astype(jnp.float32)
    spread = offsets[None, :] - fraction[:, None]
    return (jnp.sinc(spread) * jnp.sinc(spread / 3.0)).astype(jnp.bfloat16)


def kernel_table():
    support = jnp.arange(-RADIUS, RADIUS + 1).astype(jnp.float32)
    narrow = jnp.exp(-support * support / 4.5)
    slope = support * jnp.exp(-support * support / 12.5)
    broad = jnp.exp(-support * support / 40.5)
    return jnp.stack(
        [narrow / jnp.sum(narrow), slope / jnp.sum(jnp.abs(slope)), broad / jnp.sum(broad)]
    ).astype(jnp.bfloat16)


def strip_operator(taps, shift, strip_rows):
    out_rows = jnp.arange(strip_rows)[None, :, None]
    src_rows = jnp.arange(strip_rows)[None, None, :]
    offset = src_rows - out_rows - shift[:, None, None]
    table = jnp.zeros(offset.shape, jnp.bfloat16)
    for which in range(6):
        table = jnp.where(offset == which - 2, taps[:, which][:, None, None], table)
    return table


def shift_columns(values, taps, starts, width):

    def one_strip(block, tap_row, start_row):
        total = jnp.zeros((block.shape[0], width), jnp.float32)
        for which in range(6):
            moved = lax.dynamic_slice_in_dim(block, start_row[which], width, 1)
            total = total + tap_row[which].astype(jnp.float32) * moved.astype(jnp.float32)
        return total

    return jax.vmap(one_strip)(values, taps, starts)


def shift_weights(taps, shift):
    offsets = jnp.arange(-5, 7)[None, :, None]
    steps = (jnp.arange(6) - 2)[None, None, :]
    hit = offsets == shift[:, None, None] + steps
    return jnp.sum(jnp.where(hit, taps.astype(jnp.float32)[:, None, :], 0.0), axis=2)


def static_shift(values, weights, sign, width):
    wide = jnp.pad(values, ((0, 0), (0, 0), (tap_margin, tap_margin)))
    total = jnp.zeros((values.shape[0], values.shape[1], width), jnp.float32)
    for which in range(12):
        start = tap_margin + sign * (which - 5)
        moved = lax.slice_in_dim(wide, start, start + width, axis=2).astype(jnp.float32)
        total = total + weights[:, which][:, None, None] * moved
    return total


def band_operator(kernel, count):
    line = jnp.concatenate([kernel, jnp.zeros((count,), kernel.dtype)])
    width = count + 2 * RADIUS
    flat = jnp.tile(line, count)[: count * width]
    return flat.reshape(count, width)


def body(science, template, owners, patch_strip, shifts, fractions, coefs):
    ccd_count = lax.axis_size("ccd")
    row_count = lax.axis_size("row")
    amp_count = lax.axis_size("amp")
    band_rows = science.shape[1]
    half_cols = science.shape[2]
    strips = template.shape[3]
    strip_rows = template.shape[4]
    strip_size = strip_rows * half_cols
    capacity = max(2, strips // ccd_count)
    owner_list = owners.reshape(strips)
    strip_list = patch_strip.reshape(strips)
    earlier = jnp.arange(strips)[None, :] < jnp.arange(strips)[:, None]
    same_owner = owner_list[None, :] == owner_list[:, None]
    place_rank = jnp.sum(jnp.where(earlier & same_owner, 1, 0), axis=1).astype(jnp.int32)
    slot_index = owner_list * capacity + place_rank
    global_index = owner_list * strips + strip_list
    rows_here = lax.all_gather(template, "ccd", axis=0, tiled=True).reshape(-1, strip_size)
    labels = jnp.arange(rows_here.shape[0])
    select = (global_index[:, None] == labels[None, :]).astype(jnp.bfloat16)
    chosen = jnp.dot(select, rows_here, preferred_element_type=jnp.float32)
    chosen = chosen.astype(jnp.bfloat16)
    chosen = chosen.reshape(strips, strip_rows, half_cols)
    row_taps = lanczos_taps(fractions[0, 0, 0, 0])
    col_taps = lanczos_taps(fractions[0, 0, 0, 1])
    row_shift = shifts[0, 0, 0, 0]
    col_shift = shifts[0, 0, 0, 1]
    tap_steps = jnp.arange(6) - 2
    row_warp = strip_operator(row_taps, row_shift, strip_rows)
    rows_done = jnp.einsum(
        "qik,qkz->qiz", row_warp, chosen, preferred_element_type=jnp.float32
    ).astype(jnp.bfloat16)
    rows_done = lax.optimization_barrier(rows_done)
    col_weights = shift_weights(col_taps, col_shift)
    warped = static_shift(rows_done, col_weights, 1, half_cols).astype(jnp.bfloat16)
    image = warped.reshape(band_rows, half_cols)
    padded = padded_2(image, (("row", 0), ("amp", 1)), RADIUS)
    row_place = (
        (lax.axis_index("row") * band_rows + jnp.arange(band_rows) + 0.5)
        / (band_rows * row_count)
        * 2.0
        - 1.0
    )[:, None]
    col_place = (
        (lax.axis_index("amp") * half_cols + jnp.arange(half_cols) + 0.5)
        / (half_cols * amp_count)
        * 2.0
        - 1.0
    )[None, :]
    coef_block = coefs[0]
    kernels = kernel_table()
    row_mats = jnp.concatenate([band_operator(kernels[kind], band_rows) for kind in range(3)], axis=0)
    column_mats = jnp.concatenate(
        [band_operator(kernels[kind], half_cols).T for kind in range(3)], axis=1
    )
    across_all = jnp.dot(row_mats, padded, preferred_element_type=jnp.float32).astype(jnp.bfloat16)
    terms = jnp.dot(across_all, column_mats, preferred_element_type=jnp.float32)
    col_weight = coef_block[0][:, None] + coef_block[1][:, None] * col_place
    row_weight = coef_block[2][:, None] * row_place[:, 0][None, :]
    model = jnp.zeros((band_rows, half_cols), jnp.float32)
    for first in range(3):
        for second in range(3):
            basis = first * 3 + second
            term = terms[first * band_rows:(first + 1) * band_rows, second * half_cols:(second + 1) * half_cols]
            weight = col_weight[basis][None, :] + row_weight[basis][:, None]
            model = model + weight * term
    difference = science[0] - model
    lowered = difference.astype(jnp.bfloat16).reshape(strips, strip_rows, half_cols)
    lowered = lax.optimization_barrier(lowered)
    columns_back = static_shift(lowered, col_weights, -1, half_cols).astype(jnp.bfloat16)
    contribution = jnp.einsum(
        "qik,qiz->qkz", row_warp, columns_back, preferred_element_type=jnp.float32
    )
    tagged = jnp.concatenate(
        [
            contribution.reshape(strips, strip_size),
            jnp.broadcast_to(strip_list.astype(jnp.float32)[:, None] + 1.0, (strips, 128)),
        ],
        axis=1,
    )
    outgoing_back = (
        jnp.zeros((ccd_count * capacity, strip_size + 128), jnp.float32).at[slot_index].set(tagged)
    )
    returned = lax.all_to_all(
        outgoing_back.reshape(ccd_count, capacity, strip_size + 128),
        "ccd",
        split_axis=0,
        concat_axis=0,
        tiled=True,
    )
    returned = returned.reshape(ccd_count * capacity, strip_size + 128)
    asked_flat = returned[:, strip_size].astype(jnp.int32) - 1
    owner_select = (asked_flat[:, None] == jnp.arange(strips)[None, :]).astype(jnp.float32)
    stack = jnp.einsum(
        "sp,sz->pz",
        owner_select,
        returned[:, :strip_size],
        precision=lax.Precision.HIGHEST,
    )
    return (difference[None], stack.reshape(template.shape))


def solution(mesh):
    return jax.shard_map(
        body,
        mesh=mesh,
        in_specs=(
            P(("grp", "ccd"), "row", "amp"),
            P(("grp", "ccd"), "row", "amp", None, None, None),
            P(("grp", "ccd"), "row", "amp", None, None),
            P(("grp", "ccd"), "row", "amp", None),
            P(("grp", "ccd"), "row", "amp", None, None),
            P(("grp", "ccd"), "row", "amp", None, None),
            P(("grp", "ccd"), None, None),
        ),
        out_specs=(
            P(("grp", "ccd"), "row", "amp"),
            P(("grp", "ccd"), "row", "amp", None, None, None),
        ),
        check_vma=False,
    )
```

```python
import jax
import jax.numpy as jnp
from jax import lax
from jax.sharding import PartitionSpec as P

RADIUS = 9


tap_margin = 6


def padded_2(value, sides, width):
    for axis, dim in sides:
        devices, length = (lax.axis_size(axis), value.shape[dim])
        up = [(i, (i + 1) % devices) for i in range(devices - 1)]
        down = [(j, i) for i, j in up]
        last = lax.slice_in_dim(value, length - width, length, axis=dim)
        first = lax.slice_in_dim(value, 0, width, axis=dim)
        before = lax.ppermute(last, axis, up)
        after = lax.ppermute(first, axis, down)
        value = jnp.concatenate([before, value, after], axis=dim)
    return value


def lanczos_taps(fraction):
    offsets = jnp.arange(-2, 4).astype(jnp.float32)
    spread = offsets[None, :] - fraction[:, None]
    return (jnp.sinc(spread) * jnp.sinc(spread / 3.0)).astype(jnp.bfloat16)


def kernel_table():
    support = jnp.arange(-RADIUS, RADIUS + 1).astype(jnp.float32)
    narrow = jnp.exp(-support * support / 4.5)
    slope = support * jnp.exp(-support * support / 12.5)
    broad = jnp.exp(-support * support / 40.5)
    return jnp.stack(
        [narrow / jnp.sum(narrow), slope / jnp.sum(jnp.abs(slope)), broad / jnp.sum(broad)]
    ).astype(jnp.bfloat16)


def strip_operator(taps, shift, strip_rows):
    out_rows = jnp.arange(strip_rows)[None, :, None]
    src_rows = jnp.arange(strip_rows)[None, None, :]
    offset = src_rows - out_rows - shift[:, None, None]
    table = jnp.zeros(offset.shape, jnp.bfloat16)
    for which in range(6):
        table = jnp.where(offset == which - 2, taps[:, which][:, None, None], table)
    return table


def shift_columns(values, taps, starts, width):

    def one_strip(block, tap_row, start_row):
        total = jnp.zeros((block.shape[0], width), jnp.float32)
        for which in range(6):
            moved = lax.dynamic_slice_in_dim(block, start_row[which], width, 1)
            total = total + tap_row[which].astype(jnp.float32) * moved.astype(jnp.float32)
        return total

    return jax.vmap(one_strip)(values, taps, starts)


def shift_weights(taps, shift):
    offsets = jnp.arange(-5, 7)[None, :, None]
    steps = (jnp.arange(6) - 2)[None, None, :]
    hit = offsets == shift[:, None, None] + steps
    return jnp.sum(jnp.where(hit, taps.astype(jnp.float32)[:, None, :], 0.0), axis=2)


def static_shift(values, weights, sign, width):
    wide = jnp.pad(values, ((0, 0), (0, 0), (tap_margin, tap_margin)))
    total = jnp.zeros((values.shape[0], values.shape[1], width), jnp.float32)
    for which in range(12):
        start = tap_margin + sign * (which - 5)
        moved = lax.slice_in_dim(wide, start, start + width, axis=2).astype(jnp.float32)
        total = total + weights[:, which][:, None, None] * moved
    return total


def band_operator(kernel, count):
    line = jnp.concatenate([kernel, jnp.zeros((count,), kernel.dtype)])
    width = count + 2 * RADIUS
    flat = jnp.tile(line, count)[: count * width]
    return flat.reshape(count, width)


def body(science, template, owners, patch_strip, shifts, fractions, coefs):
    ccd_count = lax.axis_size("ccd")
    row_count = lax.axis_size("row")
    amp_count = lax.axis_size("amp")
    band_rows = science.shape[1]
    half_cols = science.shape[2]
    strips = template.shape[3]
    strip_rows = template.shape[4]
    strip_size = strip_rows * half_cols
    capacity = max(2, strips // ccd_count)
    owner_list = owners.reshape(strips)
    strip_list = patch_strip.reshape(strips)
    earlier = jnp.arange(strips)[None, :] < jnp.arange(strips)[:, None]
    same_owner = owner_list[None, :] == owner_list[:, None]
    place_rank = jnp.sum(jnp.where(earlier & same_owner, 1, 0), axis=1).astype(jnp.int32)
    slot_index = owner_list * capacity + place_rank
    global_index = owner_list * strips + strip_list
    rows_here = lax.all_gather(template, "ccd", axis=0, tiled=True).reshape(-1, strip_size)
    labels = jnp.arange(rows_here.shape[0])
    select = (global_index[:, None] == labels[None, :]).astype(jnp.bfloat16)
    chosen = jnp.dot(select, rows_here, preferred_element_type=jnp.float32)
    chosen = chosen.astype(jnp.bfloat16)
    chosen = chosen.reshape(strips, strip_rows, half_cols)
    row_taps = lanczos_taps(fractions[0, 0, 0, 0])
    col_taps = lanczos_taps(fractions[0, 0, 0, 1])
    row_shift = shifts[0, 0, 0, 0]
    col_shift = shifts[0, 0, 0, 1]
    tap_steps = jnp.arange(6) - 2
    row_warp = strip_operator(row_taps, row_shift, strip_rows)
    rows_done = jnp.einsum(
        "qik,qkz->qiz", row_warp, chosen, preferred_element_type=jnp.float32
    ).astype(jnp.bfloat16)
    rows_done = lax.optimization_barrier(rows_done)
    col_weights = shift_weights(col_taps, col_shift)
    warped = static_shift(rows_done, col_weights, 1, half_cols).astype(jnp.bfloat16)
    image = warped.reshape(band_rows, half_cols)
    padded = padded_2(image, (("row", 0), ("amp", 1)), RADIUS)
    row_place = (
        (lax.axis_index("row") * band_rows + jnp.arange(band_rows) + 0.5)
        / (band_rows * row_count)
        * 2.0
        - 1.0
    )[:, None]
    col_place = (
        (lax.axis_index("amp") * half_cols + jnp.arange(half_cols) + 0.5)
        / (half_cols * amp_count)
        * 2.0
        - 1.0
    )[None, :]
    coef_block = coefs[0]
    kernels = kernel_table()
    row_mats = jnp.concatenate([band_operator(kernels[kind], band_rows) for kind in range(3)], axis=0)
    column_mats = jnp.concatenate(
        [band_operator(kernels[kind], half_cols).T for kind in range(3)], axis=1
    )
    across_all = jnp.dot(row_mats, padded, preferred_element_type=jnp.float32).astype(jnp.bfloat16)
    terms = jnp.dot(across_all, column_mats, preferred_element_type=jnp.float32)
    col_weight = coef_block[0][:, None] + coef_block[1][:, None] * col_place
    row_weight = coef_block[2][:, None] * row_place[:, 0][None, :]
    model = jnp.zeros((band_rows, half_cols), jnp.float32)
    for first in range(3):
        for second in range(3):
            basis = first * 3 + second
            term = terms[first * band_rows:(first + 1) * band_rows, second * half_cols:(second + 1) * half_cols]
            weight = col_weight[basis][None, :] + row_weight[basis][:, None]
            model = model + weight * term
    difference = science[0] - model
    lowered = difference.astype(jnp.bfloat16).reshape(strips, strip_rows, half_cols)
    lowered = lax.optimization_barrier(lowered)
    pad_cols = 128 - 15
    tag = jnp.concatenate(
        [
            row_taps,
            col_taps,
            row_shift.astype(jnp.bfloat16)[:, None],
            col_shift.astype(jnp.bfloat16)[:, None],
            (strip_list + 1).astype(jnp.bfloat16)[:, None],
            jnp.zeros((strips, pad_cols), jnp.bfloat16),
        ],
        axis=1,
    )
    payload = jnp.concatenate([lowered.reshape(strips, strip_size), tag], axis=1)
    outgoing = (
        jnp.zeros((ccd_count * capacity, strip_size + 128), jnp.bfloat16).at[slot_index].set(payload)
    )
    returned = lax.all_to_all(
        outgoing.reshape(ccd_count, capacity, strip_size + 128),
        "ccd",
        split_axis=0,
        concat_axis=0,
        tiled=True,
    )
    slots = ccd_count * capacity
    returned = returned.reshape(slots, strip_size + 128)
    got = returned[:, :strip_size].reshape(slots, strip_rows, half_cols)
    tags = returned[:, strip_size:]
    got_row_taps = tags[:, 0:6]
    got_col_taps = tags[:, 6:12]
    got_row_shift = tags[:, 12].astype(jnp.int32)
    got_col_shift = tags[:, 13].astype(jnp.int32)
    asked_flat = tags[:, 14].astype(jnp.int32) - 1
    back_weights = shift_weights(got_col_taps, got_col_shift)
    columns_back = static_shift(got, back_weights, -1, half_cols).astype(jnp.bfloat16)
    back_op = strip_operator(got_row_taps, got_row_shift, strip_rows)
    contribution = jnp.einsum(
        "qik,qiz->qkz", back_op, columns_back, preferred_element_type=jnp.float32
    )
    owner_select = (asked_flat[:, None] == jnp.arange(strips)[None, :]).astype(jnp.float32)
    stack = jnp.einsum(
        "sp,sz->pz",
        owner_select,
        contribution.reshape(slots, strip_size),
        precision=lax.Precision.HIGHEST,
    )
    return (difference[None], stack.reshape(template.shape))


def solution(mesh):
    return jax.shard_map(
        body,
        mesh=mesh,
        in_specs=(
            P(("grp", "ccd"), "row", "amp"),
            P(("grp", "ccd"), "row", "amp", None, None, None),
            P(("grp", "ccd"), "row", "amp", None, None),
            P(("grp", "ccd"), "row", "amp", None),
            P(("grp", "ccd"), "row", "amp", None, None),
            P(("grp", "ccd"), "row", "amp", None, None),
            P(("grp", "ccd"), None, None),
        ),
        out_specs=(
            P(("grp", "ccd"), "row", "amp"),
            P(("grp", "ccd"), "row", "amp", None, None, None),
        ),
        check_vma=False,
    )
```

```python
import jax
import jax.numpy as jnp
from jax import lax
from jax.sharding import PartitionSpec as P

RADIUS = 9


tap_margin = 6


def padded_2(value, sides, width):
    for axis, dim in sides:
        devices, length = (lax.axis_size(axis), value.shape[dim])
        up = [(i, (i + 1) % devices) for i in range(devices - 1)]
        down = [(j, i) for i, j in up]
        last = lax.slice_in_dim(value, length - width, length, axis=dim)
        first = lax.slice_in_dim(value, 0, width, axis=dim)
        before = lax.ppermute(last, axis, up)
        after = lax.ppermute(first, axis, down)
        value = jnp.concatenate([before, value, after], axis=dim)
    return value


def halo_once(image, width):
    rows, cols = (lax.axis_size("row"), lax.axis_size("amp"))

    def place(r, a):
        return r * cols + a

    def diagonal(block, dr, da):
        pairs = [
            (place(r, a), place(r + dr, a + da))
            for r in range(rows)
            for a in range(cols)
            if 0 <= r + dr < rows and 0 <= a + da < cols
        ]
        return lax.ppermute(block, ("row", "amp"), pairs)

    up = [(i, i + 1) for i in range(rows - 1)]
    down = [(j, i) for i, j in up]
    right = [(i, i + 1) for i in range(cols - 1)]
    left = [(j, i) for i, j in right]
    above = lax.ppermute(image[-width:], "row", up)
    below = lax.ppermute(image[:width], "row", down)
    west = lax.ppermute(image[:, -width:], "amp", right)
    east = lax.ppermute(image[:, :width], "amp", left)
    north_west = diagonal(image[-width:, -width:], 1, 1)
    north_east = diagonal(image[-width:, :width], 1, -1)
    south_west = diagonal(image[:width, -width:], -1, 1)
    south_east = diagonal(image[:width, :width], -1, -1)
    top = jnp.concatenate([north_west, above, north_east], axis=1)
    middle = jnp.concatenate([west, image, east], axis=1)
    bottom = jnp.concatenate([south_west, below, south_east], axis=1)
    return jnp.concatenate([top, middle, bottom], axis=0)


def lanczos_taps(fraction):
    offsets = jnp.arange(-2, 4).astype(jnp.float32)
    spread = offsets[None, :] - fraction[:, None]
    return (jnp.sinc(spread) * jnp.sinc(spread / 3.0)).astype(jnp.bfloat16)


def kernel_table():
    support = jnp.arange(-RADIUS, RADIUS + 1).astype(jnp.float32)
    narrow = jnp.exp(-support * support / 4.5)
    slope = support * jnp.exp(-support * support / 12.5)
    broad = jnp.exp(-support * support / 40.5)
    return jnp.stack(
        [narrow / jnp.sum(narrow), slope / jnp.sum(jnp.abs(slope)), broad / jnp.sum(broad)]
    ).astype(jnp.bfloat16)


def strip_operator(taps, shift, strip_rows):
    out_rows = jnp.arange(strip_rows)[None, :, None]
    src_rows = jnp.arange(strip_rows)[None, None, :]
    offset = src_rows - out_rows - shift[:, None, None]
    table = jnp.zeros(offset.shape, jnp.bfloat16)
    for which in range(6):
        table = jnp.where(offset == which - 2, taps[:, which][:, None, None], table)
    return table


def shift_columns(values, taps, starts, width):

    def one_strip(block, tap_row, start_row):
        total = jnp.zeros((block.shape[0], width), jnp.float32)
        for which in range(6):
            moved = lax.dynamic_slice_in_dim(block, start_row[which], width, 1)
            total = total + tap_row[which].astype(jnp.float32) * moved.astype(jnp.float32)
        return total

    return jax.vmap(one_strip)(values, taps, starts)


def shift_weights(taps, shift):
    offsets = jnp.arange(-5, 7)[None, :, None]
    steps = (jnp.arange(6) - 2)[None, None, :]
    hit = offsets == shift[:, None, None] + steps
    return jnp.sum(jnp.where(hit, taps.astype(jnp.float32)[:, None, :], 0.0), axis=2)


def static_shift(values, weights, sign, width):
    wide = jnp.pad(values, ((0, 0), (0, 0), (tap_margin, tap_margin)))
    total = jnp.zeros((values.shape[0], values.shape[1], width), jnp.float32)
    for which in range(12):
        start = tap_margin + sign * (which - 5)
        moved = lax.slice_in_dim(wide, start, start + width, axis=2).astype(jnp.float32)
        total = total + weights[:, which][:, None, None] * moved
    return total


def band_operator(kernel, count):
    line = jnp.concatenate([kernel, jnp.zeros((count,), kernel.dtype)])
    width = count + 2 * RADIUS
    flat = jnp.tile(line, count)[: count * width]
    return flat.reshape(count, width)


def body(science, template, owners, patch_strip, shifts, fractions, coefs):
    ccd_count = lax.axis_size("ccd")
    row_count = lax.axis_size("row")
    amp_count = lax.axis_size("amp")
    band_rows = science.shape[1]
    half_cols = science.shape[2]
    strips = template.shape[3]
    strip_rows = template.shape[4]
    strip_size = strip_rows * half_cols
    capacity = max(2, strips // ccd_count)
    owner_list = owners.reshape(strips)
    strip_list = patch_strip.reshape(strips)
    earlier = jnp.arange(strips)[None, :] < jnp.arange(strips)[:, None]
    same_owner = owner_list[None, :] == owner_list[:, None]
    place_rank = jnp.sum(jnp.where(earlier & same_owner, 1, 0), axis=1).astype(jnp.int32)
    slot_index = owner_list * capacity + place_rank
    global_index = owner_list * strips + strip_list
    rows_here = lax.all_gather(template, "ccd", axis=0, tiled=True).reshape(-1, strip_size)
    labels = jnp.arange(rows_here.shape[0])
    select = (global_index[:, None] == labels[None, :]).astype(jnp.bfloat16)
    chosen = jnp.dot(select, rows_here, preferred_element_type=jnp.float32)
    chosen = chosen.astype(jnp.bfloat16)
    chosen = chosen.reshape(strips, strip_rows, half_cols)
    row_taps = lanczos_taps(fractions[0, 0, 0, 0])
    col_taps = lanczos_taps(fractions[0, 0, 0, 1])
    row_shift = shifts[0, 0, 0, 0]
    col_shift = shifts[0, 0, 0, 1]
    tap_steps = jnp.arange(6) - 2
    row_warp = strip_operator(row_taps, row_shift, strip_rows)
    rows_done = jnp.einsum(
        "qik,qkz->qiz", row_warp, chosen, preferred_element_type=jnp.float32
    ).astype(jnp.bfloat16)
    rows_done = lax.optimization_barrier(rows_done)
    col_weights = shift_weights(col_taps, col_shift)
    warped = static_shift(rows_done, col_weights, 1, half_cols).astype(jnp.bfloat16)
    image = warped.reshape(band_rows, half_cols)
    padded = halo_once(image, RADIUS)
    row_place = (
        (lax.axis_index("row") * band_rows + jnp.arange(band_rows) + 0.5)
        / (band_rows * row_count)
        * 2.0
        - 1.0
    )[:, None]
    col_place = (
        (lax.axis_index("amp") * half_cols + jnp.arange(half_cols) + 0.5)
        / (half_cols * amp_count)
        * 2.0
        - 1.0
    )[None, :]
    coef_block = coefs[0]
    kernels = kernel_table()
    row_mats = jnp.concatenate([band_operator(kernels[kind], band_rows) for kind in range(3)], axis=0)
    column_mats = jnp.concatenate(
        [band_operator(kernels[kind], half_cols).T for kind in range(3)], axis=1
    )
    across_all = jnp.dot(row_mats, padded, preferred_element_type=jnp.float32).astype(jnp.bfloat16)
    terms = jnp.dot(across_all, column_mats, preferred_element_type=jnp.float32)
    col_weight = coef_block[0][:, None] + coef_block[1][:, None] * col_place
    row_weight = coef_block[2][:, None] * row_place[:, 0][None, :]
    model = jnp.zeros((band_rows, half_cols), jnp.float32)
    for first in range(3):
        for second in range(3):
            basis = first * 3 + second
            term = terms[first * band_rows:(first + 1) * band_rows, second * half_cols:(second + 1) * half_cols]
            weight = col_weight[basis][None, :] + row_weight[basis][:, None]
            model = model + weight * term
    difference = science[0] - model
    lowered = difference.astype(jnp.bfloat16).reshape(strips, strip_rows, half_cols)
    lowered = lax.optimization_barrier(lowered)
    pad_cols = 128 - 15
    tag = jnp.concatenate(
        [
            row_taps,
            col_taps,
            row_shift.astype(jnp.bfloat16)[:, None],
            col_shift.astype(jnp.bfloat16)[:, None],
            (strip_list + 1).astype(jnp.bfloat16)[:, None],
            jnp.zeros((strips, pad_cols), jnp.bfloat16),
        ],
        axis=1,
    )
    payload = jnp.concatenate([lowered.reshape(strips, strip_size), tag], axis=1)
    outgoing = (
        jnp.zeros((ccd_count * capacity, strip_size + 128), jnp.bfloat16).at[slot_index].set(payload)
    )
    returned = lax.all_to_all(
        outgoing.reshape(ccd_count, capacity, strip_size + 128),
        "ccd",
        split_axis=0,
        concat_axis=0,
        tiled=True,
    )
    slots = ccd_count * capacity
    returned = returned.reshape(slots, strip_size + 128)
    got = returned[:, :strip_size].reshape(slots, strip_rows, half_cols)
    tags = returned[:, strip_size:]
    got_row_taps = tags[:, 0:6]
    got_col_taps = tags[:, 6:12]
    got_row_shift = tags[:, 12].astype(jnp.int32)
    got_col_shift = tags[:, 13].astype(jnp.int32)
    asked_flat = tags[:, 14].astype(jnp.int32) - 1
    back_weights = shift_weights(got_col_taps, got_col_shift)
    columns_back = static_shift(got, back_weights, -1, half_cols).astype(jnp.bfloat16)
    back_op = strip_operator(got_row_taps, got_row_shift, strip_rows)
    contribution = jnp.einsum(
        "qik,qiz->qkz", back_op, columns_back, preferred_element_type=jnp.float32
    )
    owner_select = (asked_flat[:, None] == jnp.arange(strips)[None, :]).astype(jnp.float32)
    stack = jnp.einsum(
        "sp,sz->pz",
        owner_select,
        contribution.reshape(slots, strip_size),
        precision=lax.Precision.HIGHEST,
    )
    return (difference[None], stack.reshape(template.shape))


def solution(mesh):
    return jax.shard_map(
        body,
        mesh=mesh,
        in_specs=(
            P(("grp", "ccd"), "row", "amp"),
            P(("grp", "ccd"), "row", "amp", None, None, None),
            P(("grp", "ccd"), "row", "amp", None, None),
            P(("grp", "ccd"), "row", "amp", None),
            P(("grp", "ccd"), "row", "amp", None, None),
            P(("grp", "ccd"), "row", "amp", None, None),
            P(("grp", "ccd"), None, None),
        ),
        out_specs=(
            P(("grp", "ccd"), "row", "amp"),
            P(("grp", "ccd"), "row", "amp", None, None, None),
        ),
        check_vma=False,
    )
```

```python
import jax
import jax.numpy as jnp
from jax import lax
from jax.sharding import PartitionSpec as P

RADIUS = 9


tap_margin = 6


def padded_2(value, sides, width):
    for axis, dim in sides:
        devices, length = (lax.axis_size(axis), value.shape[dim])
        up = [(i, (i + 1) % devices) for i in range(devices - 1)]
        down = [(j, i) for i, j in up]
        last = lax.slice_in_dim(value, length - width, length, axis=dim)
        first = lax.slice_in_dim(value, 0, width, axis=dim)
        before = lax.ppermute(last, axis, up)
        after = lax.ppermute(first, axis, down)
        value = jnp.concatenate([before, value, after], axis=dim)
    return value


def halo_once(image, width):
    rows, cols = (lax.axis_size("row"), lax.axis_size("amp"))

    def place(r, a):
        return r * cols + a

    def diagonal(block, dr, da):
        pairs = [
            (place(r, a), place(r + dr, a + da))
            for r in range(rows)
            for a in range(cols)
            if 0 <= r + dr < rows and 0 <= a + da < cols
        ]
        return lax.ppermute(block, ("row", "amp"), pairs)

    up = [(i, i + 1) for i in range(rows - 1)]
    down = [(j, i) for i, j in up]
    right = [(i, i + 1) for i in range(cols - 1)]
    left = [(j, i) for i, j in right]
    above = lax.ppermute(image[-width:], "row", up)
    below = lax.ppermute(image[:width], "row", down)
    west = lax.ppermute(image[:, -width:], "amp", right)
    east = lax.ppermute(image[:, :width], "amp", left)
    north_west = diagonal(image[-width:, -width:], 1, 1)
    north_east = diagonal(image[-width:, :width], 1, -1)
    south_west = diagonal(image[:width, -width:], -1, 1)
    south_east = diagonal(image[:width, :width], -1, -1)
    top = jnp.concatenate([north_west, above, north_east], axis=1)
    middle = jnp.concatenate([west, image, east], axis=1)
    bottom = jnp.concatenate([south_west, below, south_east], axis=1)
    return jnp.concatenate([top, middle, bottom], axis=0)


def lanczos_taps(fraction):
    offsets = jnp.arange(-2, 4).astype(jnp.float32)
    spread = offsets[None, :] - fraction[:, None]
    return (jnp.sinc(spread) * jnp.sinc(spread / 3.0)).astype(jnp.bfloat16)


def kernel_table():
    support = jnp.arange(-RADIUS, RADIUS + 1).astype(jnp.float32)
    narrow = jnp.exp(-support * support / 4.5)
    slope = support * jnp.exp(-support * support / 12.5)
    broad = jnp.exp(-support * support / 40.5)
    return jnp.stack(
        [narrow / jnp.sum(narrow), slope / jnp.sum(jnp.abs(slope)), broad / jnp.sum(broad)]
    ).astype(jnp.bfloat16)


def strip_operator(taps, shift, strip_rows):
    out_rows = jnp.arange(strip_rows)[None, :, None]
    src_rows = jnp.arange(strip_rows)[None, None, :]
    offset = src_rows - out_rows - shift[:, None, None]
    table = jnp.zeros(offset.shape, jnp.bfloat16)
    for which in range(6):
        table = jnp.where(offset == which - 2, taps[:, which][:, None, None], table)
    return table


def shift_columns(values, taps, starts, width):

    def one_strip(block, tap_row, start_row):
        total = jnp.zeros((block.shape[0], width), jnp.float32)
        for which in range(6):
            moved = lax.dynamic_slice_in_dim(block, start_row[which], width, 1)
            total = total + tap_row[which].astype(jnp.float32) * moved.astype(jnp.float32)
        return total

    return jax.vmap(one_strip)(values, taps, starts)


def shift_weights(taps, shift):
    offsets = jnp.arange(-5, 7)[None, :, None]
    steps = (jnp.arange(6) - 2)[None, None, :]
    hit = offsets == shift[:, None, None] + steps
    return jnp.sum(jnp.where(hit, taps.astype(jnp.float32)[:, None, :], 0.0), axis=2)


def static_shift(values, weights, sign, width):
    wide = jnp.pad(values, ((0, 0), (0, 0), (tap_margin, tap_margin)))
    total = jnp.zeros((values.shape[0], values.shape[1], width), jnp.float32)
    for which in range(12):
        start = tap_margin + sign * (which - 5)
        moved = lax.slice_in_dim(wide, start, start + width, axis=2).astype(jnp.float32)
        total = total + weights[:, which][:, None, None] * moved
    return total


def band_operator(kernel, count):
    line = jnp.concatenate([kernel, jnp.zeros((count,), kernel.dtype)])
    width = count + 2 * RADIUS
    flat = jnp.tile(line, count)[: count * width]
    return flat.reshape(count, width)


def body(science, template, owners, patch_strip, shifts, fractions, coefs):
    ccd_count = lax.axis_size("ccd")
    row_count = lax.axis_size("row")
    amp_count = lax.axis_size("amp")
    band_rows = science.shape[1]
    half_cols = science.shape[2]
    strips = template.shape[3]
    strip_rows = template.shape[4]
    strip_size = strip_rows * half_cols
    capacity = max(2, strips // ccd_count)
    owner_list = owners.reshape(strips)
    strip_list = patch_strip.reshape(strips)
    earlier = jnp.arange(strips)[None, :] < jnp.arange(strips)[:, None]
    same_owner = owner_list[None, :] == owner_list[:, None]
    place_rank = jnp.sum(jnp.where(earlier & same_owner, 1, 0), axis=1).astype(jnp.int32)
    slot_index = owner_list * capacity + place_rank
    slot_match = jnp.arange(ccd_count * capacity)[:, None] == slot_index[None, :]
    wanted = jnp.sum(jnp.where(slot_match, strip_list[None, :] + 1, 0), axis=1) - 1
    asked = lax.all_to_all(
        wanted.reshape(ccd_count, capacity), "ccd", split_axis=0, concat_axis=0, tiled=True
    ).reshape(ccd_count * capacity)
    own_rows = template.reshape(strips, strip_size)
    give = (asked[:, None] == jnp.arange(strips)[None, :]).astype(jnp.bfloat16)
    sending = jnp.dot(give, own_rows, preferred_element_type=jnp.float32).astype(jnp.bfloat16)
    fetched = lax.all_to_all(
        sending.reshape(ccd_count, capacity, strip_size), "ccd", split_axis=0, concat_axis=0, tiled=True
    ).reshape(ccd_count * capacity, strip_size)
    select = slot_match.astype(jnp.bfloat16)
    chosen = jnp.dot(select.T, fetched, preferred_element_type=jnp.float32)
    chosen = chosen.astype(jnp.bfloat16)
    chosen = chosen.reshape(strips, strip_rows, half_cols)
    row_taps = lanczos_taps(fractions[0, 0, 0, 0])
    col_taps = lanczos_taps(fractions[0, 0, 0, 1])
    row_shift = shifts[0, 0, 0, 0]
    col_shift = shifts[0, 0, 0, 1]
    tap_steps = jnp.arange(6) - 2
    row_warp = strip_operator(row_taps, row_shift, strip_rows)
    rows_done = jnp.einsum(
        "qik,qkz->qiz", row_warp, chosen, preferred_element_type=jnp.float32
    ).astype(jnp.bfloat16)
    rows_done = lax.optimization_barrier(rows_done)
    col_weights = shift_weights(col_taps, col_shift)
    warped = static_shift(rows_done, col_weights, 1, half_cols).astype(jnp.bfloat16)
    image = warped.reshape(band_rows, half_cols)
    padded = halo_once(image, RADIUS)
    row_place = (
        (lax.axis_index("row") * band_rows + jnp.arange(band_rows) + 0.5)
        / (band_rows * row_count)
        * 2.0
        - 1.0
    )[:, None]
    col_place = (
        (lax.axis_index("amp") * half_cols + jnp.arange(half_cols) + 0.5)
        / (half_cols * amp_count)
        * 2.0
        - 1.0
    )[None, :]
    coef_block = coefs[0]
    kernels = kernel_table()
    row_mats = jnp.concatenate([band_operator(kernels[kind], band_rows) for kind in range(3)], axis=0)
    column_mats = jnp.concatenate(
        [band_operator(kernels[kind], half_cols).T for kind in range(3)], axis=1
    )
    across_all = jnp.dot(row_mats, padded, preferred_element_type=jnp.float32).astype(jnp.bfloat16)
    terms = jnp.dot(across_all, column_mats, preferred_element_type=jnp.float32)
    col_weight = coef_block[0][:, None] + coef_block[1][:, None] * col_place
    row_weight = coef_block[2][:, None] * row_place[:, 0][None, :]
    model = jnp.zeros((band_rows, half_cols), jnp.float32)
    for first in range(3):
        for second in range(3):
            basis = first * 3 + second
            term = terms[first * band_rows:(first + 1) * band_rows, second * half_cols:(second + 1) * half_cols]
            weight = col_weight[basis][None, :] + row_weight[basis][:, None]
            model = model + weight * term
    difference = science[0] - model
    lowered = difference.astype(jnp.bfloat16).reshape(strips, strip_rows, half_cols)
    lowered = lax.optimization_barrier(lowered)
    pad_cols = 128 - 15
    tag = jnp.concatenate(
        [
            row_taps,
            col_taps,
            row_shift.astype(jnp.bfloat16)[:, None],
            col_shift.astype(jnp.bfloat16)[:, None],
            (strip_list + 1).astype(jnp.bfloat16)[:, None],
            jnp.zeros((strips, pad_cols), jnp.bfloat16),
        ],
        axis=1,
    )
    payload = jnp.concatenate([lowered.reshape(strips, strip_size), tag], axis=1)
    outgoing = (
        jnp.zeros((ccd_count * capacity, strip_size + 128), jnp.bfloat16).at[slot_index].set(payload)
    )
    returned = lax.all_to_all(
        outgoing.reshape(ccd_count, capacity, strip_size + 128),
        "ccd",
        split_axis=0,
        concat_axis=0,
        tiled=True,
    )
    slots = ccd_count * capacity
    returned = returned.reshape(slots, strip_size + 128)
    got = returned[:, :strip_size].reshape(slots, strip_rows, half_cols)
    tags = returned[:, strip_size:]
    got_row_taps = tags[:, 0:6]
    got_col_taps = tags[:, 6:12]
    got_row_shift = tags[:, 12].astype(jnp.int32)
    got_col_shift = tags[:, 13].astype(jnp.int32)
    asked_flat = tags[:, 14].astype(jnp.int32) - 1
    back_weights = shift_weights(got_col_taps, got_col_shift)
    columns_back = static_shift(got, back_weights, -1, half_cols).astype(jnp.bfloat16)
    back_op = strip_operator(got_row_taps, got_row_shift, strip_rows)
    contribution = jnp.einsum(
        "qik,qiz->qkz", back_op, columns_back, preferred_element_type=jnp.float32
    )
    owner_select = (asked_flat[:, None] == jnp.arange(strips)[None, :]).astype(jnp.float32)
    stack = jnp.einsum(
        "sp,sz->pz",
        owner_select,
        contribution.reshape(slots, strip_size),
        precision=lax.Precision.HIGHEST,
    )
    return (difference[None], stack.reshape(template.shape))


def solution(mesh):
    return jax.shard_map(
        body,
        mesh=mesh,
        in_specs=(
            P(("grp", "ccd"), "row", "amp"),
            P(("grp", "ccd"), "row", "amp", None, None, None),
            P(("grp", "ccd"), "row", "amp", None, None),
            P(("grp", "ccd"), "row", "amp", None),
            P(("grp", "ccd"), "row", "amp", None, None),
            P(("grp", "ccd"), "row", "amp", None, None),
            P(("grp", "ccd"), None, None),
        ),
        out_specs=(
            P(("grp", "ccd"), "row", "amp"),
            P(("grp", "ccd"), "row", "amp", None, None, None),
        ),
        check_vma=False,
    )
```

```python
import jax
import jax.numpy as jnp
from jax import lax
from jax.sharding import PartitionSpec as P

RADIUS = 9


tap_margin = 6


def padded_2(value, sides, width):
    for axis, dim in sides:
        devices, length = (lax.axis_size(axis), value.shape[dim])
        up = [(i, (i + 1) % devices) for i in range(devices - 1)]
        down = [(j, i) for i, j in up]
        last = lax.slice_in_dim(value, length - width, length, axis=dim)
        first = lax.slice_in_dim(value, 0, width, axis=dim)
        before = lax.ppermute(last, axis, up)
        after = lax.ppermute(first, axis, down)
        value = jnp.concatenate([before, value, after], axis=dim)
    return value


def halo_once(image, width):
    rows, cols = (lax.axis_size("row"), lax.axis_size("amp"))

    def place(r, a):
        return r * cols + a

    def diagonal(block, dr, da):
        pairs = [
            (place(r, a), place(r + dr, a + da))
            for r in range(rows)
            for a in range(cols)
            if 0 <= r + dr < rows and 0 <= a + da < cols
        ]
        return lax.ppermute(block, ("row", "amp"), pairs)

    up = [(i, i + 1) for i in range(rows - 1)]
    down = [(j, i) for i, j in up]
    right = [(i, i + 1) for i in range(cols - 1)]
    left = [(j, i) for i, j in right]
    above = lax.ppermute(image[-width:], "row", up)
    below = lax.ppermute(image[:width], "row", down)
    west = lax.ppermute(image[:, -width:], "amp", right)
    east = lax.ppermute(image[:, :width], "amp", left)
    north_west = diagonal(image[-width:, -width:], 1, 1)
    north_east = diagonal(image[-width:, :width], 1, -1)
    south_west = diagonal(image[:width, -width:], -1, 1)
    south_east = diagonal(image[:width, :width], -1, -1)
    top = jnp.concatenate([north_west, above, north_east], axis=1)
    middle = jnp.concatenate([west, image, east], axis=1)
    bottom = jnp.concatenate([south_west, below, south_east], axis=1)
    return jnp.concatenate([top, middle, bottom], axis=0)


def lanczos_taps(fraction):
    offsets = jnp.arange(-2, 4).astype(jnp.float32)
    spread = offsets[None, :] - fraction[:, None]
    return (jnp.sinc(spread) * jnp.sinc(spread / 3.0)).astype(jnp.bfloat16)


def kernel_table():
    support = jnp.arange(-RADIUS, RADIUS + 1).astype(jnp.float32)
    narrow = jnp.exp(-support * support / 4.5)
    slope = support * jnp.exp(-support * support / 12.5)
    broad = jnp.exp(-support * support / 40.5)
    return jnp.stack(
        [narrow / jnp.sum(narrow), slope / jnp.sum(jnp.abs(slope)), broad / jnp.sum(broad)]
    ).astype(jnp.bfloat16)


def strip_operator(taps, shift, strip_rows):
    out_rows = jnp.arange(strip_rows)[None, :, None]
    src_rows = jnp.arange(strip_rows)[None, None, :]
    offset = src_rows - out_rows - shift[:, None, None]
    table = jnp.zeros(offset.shape, jnp.bfloat16)
    for which in range(6):
        table = jnp.where(offset == which - 2, taps[:, which][:, None, None], table)
    return table


def shift_columns(values, taps, starts, width):

    def one_strip(block, tap_row, start_row):
        total = jnp.zeros((block.shape[0], width), jnp.float32)
        for which in range(6):
            moved = lax.dynamic_slice_in_dim(block, start_row[which], width, 1)
            total = total + tap_row[which].astype(jnp.float32) * moved.astype(jnp.float32)
        return total

    return jax.vmap(one_strip)(values, taps, starts)


def shift_weights(taps, shift):
    offsets = jnp.arange(-5, 7)[None, :, None]
    steps = (jnp.arange(6) - 2)[None, None, :]
    hit = offsets == shift[:, None, None] + steps
    return jnp.sum(jnp.where(hit, taps.astype(jnp.float32)[:, None, :], 0.0), axis=2)


def static_shift(values, weights, sign, width):
    wide = jnp.pad(values, ((0, 0), (0, 0), (tap_margin, tap_margin)))
    total = jnp.zeros((values.shape[0], values.shape[1], width), jnp.float32)
    for which in range(12):
        start = tap_margin + sign * (which - 5)
        moved = lax.slice_in_dim(wide, start, start + width, axis=2).astype(jnp.float32)
        total = total + weights[:, which][:, None, None] * moved
    return total


def band_operator(kernel, count):
    line = jnp.concatenate([kernel, jnp.zeros((count,), kernel.dtype)])
    width = count + 2 * RADIUS
    flat = jnp.tile(line, count)[: count * width]
    return flat.reshape(count, width)


def body(science, template, owners, patch_strip, shifts, fractions, coefs):
    ccd_count = lax.axis_size("ccd")
    row_count = lax.axis_size("row")
    amp_count = lax.axis_size("amp")
    band_rows = science.shape[1]
    half_cols = science.shape[2]
    strips = template.shape[3]
    strip_rows = template.shape[4]
    strip_size = strip_rows * half_cols
    capacity = max(2, strips // ccd_count)
    owner_list = owners.reshape(strips)
    strip_list = patch_strip.reshape(strips)
    earlier = jnp.arange(strips)[None, :] < jnp.arange(strips)[:, None]
    same_owner = owner_list[None, :] == owner_list[:, None]
    place_rank = jnp.sum(jnp.where(earlier & same_owner, 1, 0), axis=1).astype(jnp.int32)
    slot_index = owner_list * capacity + place_rank
    slot_match = jnp.arange(ccd_count * capacity)[:, None] == slot_index[None, :]
    wanted = jnp.sum(jnp.where(slot_match, strip_list[None, :] + 1, 0), axis=1) - 1
    asked = lax.all_to_all(
        wanted.reshape(ccd_count, capacity), "ccd", split_axis=0, concat_axis=0, tiled=True
    ).reshape(ccd_count * capacity)
    own_rows = template.reshape(strips, strip_size)
    give = (asked[:, None] == jnp.arange(strips)[None, :]).astype(jnp.bfloat16)
    sending = jnp.dot(give, own_rows, preferred_element_type=jnp.float32).astype(jnp.bfloat16)
    fetched = lax.all_to_all(
        sending.reshape(ccd_count, capacity, strip_size), "ccd", split_axis=0, concat_axis=0, tiled=True
    ).reshape(ccd_count * capacity, strip_size)
    select = slot_match.astype(jnp.bfloat16)
    chosen = jnp.dot(select.T, fetched, preferred_element_type=jnp.float32)
    chosen = chosen.astype(jnp.bfloat16)
    chosen = chosen.reshape(strips, strip_rows, half_cols)
    row_taps = lanczos_taps(fractions[0, 0, 0, 0])
    col_taps = lanczos_taps(fractions[0, 0, 0, 1])
    row_shift = shifts[0, 0, 0, 0]
    col_shift = shifts[0, 0, 0, 1]
    tap_steps = jnp.arange(6) - 2
    row_warp = strip_operator(row_taps, row_shift, strip_rows)
    rows_done = jnp.einsum(
        "qik,qkz->qiz", row_warp, chosen, preferred_element_type=jnp.float32
    ).astype(jnp.bfloat16)
    col_weights = shift_weights(col_taps, col_shift)
    warped = static_shift(rows_done, col_weights, 1, half_cols).astype(jnp.bfloat16)
    image = warped.reshape(band_rows, half_cols)
    padded = halo_once(image, RADIUS)
    row_place = (
        (lax.axis_index("row") * band_rows + jnp.arange(band_rows) + 0.5)
        / (band_rows * row_count)
        * 2.0
        - 1.0
    )[:, None]
    col_place = (
        (lax.axis_index("amp") * half_cols + jnp.arange(half_cols) + 0.5)
        / (half_cols * amp_count)
        * 2.0
        - 1.0
    )[None, :]
    coef_block = coefs[0]
    kernels = kernel_table()
    row_mats = jnp.concatenate([band_operator(kernels[kind], band_rows) for kind in range(3)], axis=0)
    column_mats = jnp.concatenate(
        [band_operator(kernels[kind], half_cols).T for kind in range(3)], axis=1
    )
    across_all = jnp.dot(row_mats, padded, preferred_element_type=jnp.float32).astype(jnp.bfloat16)
    terms = jnp.dot(across_all, column_mats, preferred_element_type=jnp.float32)
    col_weight = coef_block[0][:, None] + coef_block[1][:, None] * col_place
    row_weight = coef_block[2][:, None] * row_place[:, 0][None, :]
    model = jnp.zeros((band_rows, half_cols), jnp.float32)
    for first in range(3):
        for second in range(3):
            basis = first * 3 + second
            term = terms[first * band_rows:(first + 1) * band_rows, second * half_cols:(second + 1) * half_cols]
            weight = col_weight[basis][None, :] + row_weight[basis][:, None]
            model = model + weight * term
    difference = science[0] - model
    lowered = difference.astype(jnp.bfloat16).reshape(strips, strip_rows, half_cols)
    lowered = lax.optimization_barrier(lowered)
    pad_cols = 128 - 15
    tag = jnp.concatenate(
        [
            row_taps,
            col_taps,
            row_shift.astype(jnp.bfloat16)[:, None],
            col_shift.astype(jnp.bfloat16)[:, None],
            (strip_list + 1).astype(jnp.bfloat16)[:, None],
            jnp.zeros((strips, pad_cols), jnp.bfloat16),
        ],
        axis=1,
    )
    payload = jnp.concatenate([lowered.reshape(strips, strip_size), tag], axis=1)
    outgoing = (
        jnp.zeros((ccd_count * capacity, strip_size + 128), jnp.bfloat16).at[slot_index].set(payload)
    )
    returned = lax.all_to_all(
        outgoing.reshape(ccd_count, capacity, strip_size + 128),
        "ccd",
        split_axis=0,
        concat_axis=0,
        tiled=True,
    )
    slots = ccd_count * capacity
    returned = returned.reshape(slots, strip_size + 128)
    got = returned[:, :strip_size].reshape(slots, strip_rows, half_cols)
    tags = returned[:, strip_size:]
    got_row_taps = tags[:, 0:6]
    got_col_taps = tags[:, 6:12]
    got_row_shift = tags[:, 12].astype(jnp.int32)
    got_col_shift = tags[:, 13].astype(jnp.int32)
    asked_flat = tags[:, 14].astype(jnp.int32) - 1
    back_weights = shift_weights(got_col_taps, got_col_shift)
    columns_back = static_shift(got, back_weights, -1, half_cols).astype(jnp.bfloat16)
    back_op = strip_operator(got_row_taps, got_row_shift, strip_rows)
    contribution = jnp.einsum(
        "qik,qiz->qkz", back_op, columns_back, preferred_element_type=jnp.float32
    )
    owner_select = (asked_flat[:, None] == jnp.arange(strips)[None, :]).astype(jnp.float32)
    stack = jnp.einsum(
        "sp,sz->pz",
        owner_select,
        contribution.reshape(slots, strip_size),
        precision=lax.Precision.HIGHEST,
    )
    return (difference[None], stack.reshape(template.shape))


def solution(mesh):
    return jax.shard_map(
        body,
        mesh=mesh,
        in_specs=(
            P(("grp", "ccd"), "row", "amp"),
            P(("grp", "ccd"), "row", "amp", None, None, None),
            P(("grp", "ccd"), "row", "amp", None, None),
            P(("grp", "ccd"), "row", "amp", None),
            P(("grp", "ccd"), "row", "amp", None, None),
            P(("grp", "ccd"), "row", "amp", None, None),
            P(("grp", "ccd"), None, None),
        ),
        out_specs=(
            P(("grp", "ccd"), "row", "amp"),
            P(("grp", "ccd"), "row", "amp", None, None, None),
        ),
        check_vma=False,
    )
```
